128 devices in a mesh: ka: 64 (over y, z, x_lo, core), pa: 2 (over x_hi).
Axes of the slice: x: 4 (x_hi: 2, x_lo: 2; x = x_hi * 2 + x_lo), y: 4, z: 4, core: 2. Of those that a mesh axis runs over, the one named last changes fastest.
Arguments:
- conduction: bfloat16 [64, 48, 2048], P('ka'), may hold values from -6 to 6
- weighted: bfloat16 [64, 48, 2048], P('ka'), may hold values from -6 to 6
- valence: bfloat16 [64, 64, 2048], P('ka', None, 'pa'), may hold values from -0.015625 to 0.015625
- screening: bfloat16 [64, 2048, 2048], P('ka', None, 'pa'), may hold values from -0.125 to 0.125
- pair_transfer: int32 [64, 64], replicated, may hold values from 0 to 63, as said below
- owner_map: int32 [64], replicated, may hold values from 0 to 63, each once
Outputs:
- kernel_out: float32 [64, 48, 64], P('ka')
The draws below stay inside these ranges and needn't reach their ends.
Inputs may be any that keep to these rules, and one draw needn't show every extreme that they name: pair_transfer[i, j] = (g_i - g_j) mod 64 for positions g of the k-points on a cyclic grid of 64 points (a permutation drawn from the seed), so each row and each column names every transfer once. `owner_map`: each transfer is held by exactly one slot.
All inputs are finite; a program needn't handle non-finite values.
Results may differ from the reference program's by a relative error of at most 0.0029.
Values may be sent and summed in bfloat16 or wider, within the bound.
No kernel may reach another device: no remote copies, remote signals or barrier semaphores. Data moves between devices by JAX's collectives and lax.ppermute only.
A program may use at most 128 MiB of HBM per device.

```python
import jax
import jax.numpy as jnp
from jax import lax

NB = 48
NV = 64
P_SIZE = 2048
NK = 64


def draw_pair_transfer(key, part):
    positions = jax.random.permutation(jax.random.fold_in(key, 11), NK)
    return jnp.mod(positions[:, None] - positions[None, :], NK).astype(jnp.int32)


def level_of(own_key, extent, split, least, high):
    def one(position, shards_of):
        steps = jax.random.uniform(jax.random.fold_in(jax.random.fold_in(own_key, 6), position), (shards_of,), jnp.float32, least / len(split), high / len(split))
        return jnp.repeat(jnp.exp(steps), extent[position] // shards_of).reshape((-1,) + (1,) * (len(extent) - position - 1))

    factor_of = one(*split[0])
    for cut in split[1:]:
        factor_of = factor_of * one(*cut)
    return factor_of


def noise(stream_key, dims, deviation, bound, pieces=(), held_as=jnp.bfloat16):
    array = deviation * jax.random.normal(stream_key, dims, jnp.float32)
    if pieces:
        array = array * level_of(stream_key, dims, pieces, -0.22, 0.18)
    return jnp.clip(array, -bound, bound).astype(held_as)


def setup_inputs(seed: int = 0) -> dict:
    streams_of = jax.random.split(jax.random.key(seed), 7)
    return {
        "conduction": noise(streams_of[0], (NK, NB, P_SIZE), 1.0, 6.0, ((0, 64),)),
        "weighted": noise(streams_of[1], (NK, NB, P_SIZE), 1.0, 6.0, ((0, 64),)),
        "valence": noise(streams_of[2], (NK, NV, P_SIZE), (P_SIZE * NK) ** -0.5, 0.015625, ((0, 64), (2, 2))),
        "screening": noise(streams_of[3], (NK, P_SIZE, P_SIZE), P_SIZE ** -0.5, 0.125, ((0, 64), (2, 2))),
        "pair_transfer": draw_pair_transfer(jax.random.fold_in(streams_of[6], 71), 0),
        "owner_map": jax.random.permutation(streams_of[5], NK).astype(jnp.int32),
    }


def reference(conduction, weighted, valence, screening, pair_transfer, owner_map):
    columns = jnp.arange(NK, dtype=jnp.int32)
    weighted_wide = weighted.astype(jnp.float32)

    def visit(total, slot):
        transfer = owner_map[slot]
        partners = jnp.sum(jnp.where(pair_transfer == transfer, columns[None, :], 0), axis=1).astype(jnp.int32)
        partner_cond = jnp.take(conduction, partners, axis=0).astype(jnp.float32)
        density = (partner_cond * weighted_wide).astype(jnp.bfloat16)
        screened = jnp.dot(density.reshape(NK * NB, P_SIZE), screening[slot], preferred_element_type=jnp.float32)
        return total + partner_cond * screened.reshape(NK, NB, P_SIZE), None

    folded, _ = lax.scan(visit, jnp.zeros((NK, NB, P_SIZE), jnp.float32), jnp.arange(NK, dtype=jnp.int32))
    return jnp.einsum("kbp,kvp->kbv", folded, valence.astype(jnp.float32), precision=lax.Precision.HIGHEST)
```

```python
import functools
import itertools

import jax
import jax.numpy as jnp
import numpy as np
from jax import lax
from jax.experimental import pallas as pl
from jax.experimental.pallas import tpu as pltpu
from jax.sharding import PartitionSpec as P


NY, NZ, NX = 4, 4, 4
CHIPS = 32
AXES = ("ka", "pa")
STEPS = {
    "y": ("y", 1, 3),
    "Y": ("y", 3, 1),
    "z": ("z", 1, 3),
    "Z": ("z", 3, 1),
    "x": ("x", 1, 3),
    "v": ("x", 1, 1),
}
SEQ = ("YZyzx", "ZYzyx", "xZYzy", "vYZyz")
TILE = 8


def device(y, z, x, core):
    return (((y * NZ + z) * 2 + x % 2) * 2 + core) * 2 + x // 2


def moved(masks):
    pairs = []
    for y, z, x, core in itertools.product(range(NY), range(NZ), range(NX), range(2)):
        my, mz, mx, mc = masks[core]
        pairs.append((device(y, z, x, core), device(y ^ my, z ^ mz, x ^ mx, core ^ mc)))
    return pairs


def send(value, masks):
    return lax.ppermute(value, AXES, moved(masks))


def step_masks(letter):
    dim, *per_core = STEPS[letter]
    return [tuple(mask if dim == name else 0 for name in "yzx") + (0,) for mask in per_core]


def core_swap(value):
    return send(value, [(0, 0, 0, 1)] * 2)


def gathered(block, seq):
    for letter in seq:
        block = jnp.concatenate([block, send(block, step_masks(letter))], axis=0)
    return block


def positions(seq):
    table = np.zeros((2, CHIPS), np.int32)
    for core in range(2):
        for place in range(CHIPS):
            off = {"y": 0, "z": 0, "x": 0}
            for bit, letter in enumerate(seq):
                if place >> bit & 1:
                    off[STEPS[letter][0]] ^= STEPS[letter][1 + core]
            table[core, off["y"] * 8 + off["z"] * 2 + (off["x"] & 1)] = place
    return table


def kernel(partner, me, place, s0, s1, s2, o0, o1, o2, val, wa, wb, out, dens, fold, total):
    chip, core, column = me[0], me[1], pl.multiple_of(me[2], 128)
    own, other = (s0, s1, s2), (o0, o1, o2)
    slots = (wa, wb)
    rows = TILE * 48

    @pl.loop(0, CHIPS // TILE)
    def _(tile):
        @pl.loop(0, TILE)
        def _(unit):
            off = tile * TILE + unit
            home = (lax.bitwise_xor(chip, off)) * 2 + core
            for part in range(3):
                weights = own[part][place[part, core, off], pl.ds(16, 16), :]
                row = pl.multiple_of(unit * 48 + 16 * part, 16)
                for slot in range(2):
                    mate = partner[slot, home]
                    mate_core = lax.rem(mate, 2)
                    mate_off = lax.bitwise_xor(lax.div(mate, 2), chip)
                    where = place[part, mate_core, mate_off]

                    def put(source):
                        mates = source[where, pl.ds(0, 16), :]
                        dens[slot, pl.ds(row, 16), :] = mates * weights
                        fold[slot, pl.ds(row, 16), :] = source[where, pl.ds(0, 16), pl.ds(column, 1024)]

                    pl.when(mate_core == core)(lambda: put(own[part]))
                    pl.when(mate_core != core)(lambda: put(other[part]))

        for cut in range(4):
            cols = pl.ds(cut * 256, 256)
            acc = None
            for slot in range(2):
                screened = jnp.dot(dens[slot], slots[slot][:, cols], preferred_element_type=jnp.float32)
                term = fold[slot, :, cols].astype(jnp.float32) * screened
                acc = term if acc is None else acc + term
            total[:, cols] = acc

        @pl.loop(0, TILE)
        def _(unit):
            off = tile * TILE + unit
            row = pl.multiple_of(unit * 48, 16)
            folded = total[pl.ds(row, 48), :]
            high = folded.astype(jnp.bfloat16)
            low = (folded - high.astype(jnp.float32)).astype(jnp.bfloat16)
            bands = val[place[3, core, off]]
            contract = (((1,), (1,)), ((), ()))
            both = lax.dot_general(
                jnp.concatenate([high, low], axis=0), bands, contract, preferred_element_type=jnp.float32
            )
            out[off] = both[:48] + both[48:]


def apply(partner, me, place, streams, others, val, wa, wb):
    vmem = pl.BlockSpec(memory_space=pltpu.VMEM)
    rows = TILE * 48
    return pl.pallas_call(
        kernel,
        grid_spec=pltpu.PrefetchScalarGridSpec(
            num_scalar_prefetch=3,
            grid=(),
            in_specs=[vmem] * 9,
            out_specs=vmem,
            scratch_shapes=[
                pltpu.VMEM((2, rows, 2048), jnp.bfloat16),
                pltpu.VMEM((2, rows, 1024), jnp.bfloat16),
                pltpu.VMEM((rows, 1024), jnp.float32),
            ],
        ),
        out_shape=jax.ShapeDtypeStruct((CHIPS, 48, 64), jnp.float32),
        compiler_params=pltpu.CompilerParams(vmem_limit_bytes=44 << 20),
        cost_estimate=pl.CostEstimate(flops=14_000_000_000, bytes_accessed=32 << 20, transcendentals=0),
    )(partner, me, place, *streams, *others, val, wa, wb)


def spread(parts, dim, masks):
    moves = []
    for mask in masks:
        one = tuple(mask if dim == name else 0 for name in "yzx") + (0,)
        moves.append(send(parts[mask], [one] * 2))
    return parts[0] + moves[0] + moves[1] + moves[2]


def shards(conduction, weighted, valence, screening, pair_transfer, owner_map):
    ka, pa = lax.axis_index("ka"), lax.axis_index("pa")
    chip, core = ka // 2, ka % 2
    owned = lax.dynamic_slice_in_dim(owner_map, chip * 2, 2)
    columns = jnp.arange(pair_transfer.shape[1], dtype=jnp.int32)
    partner = jnp.sum(jnp.where(pair_transfer[None] == owned[:, None, None], columns, 0), axis=2)
    me = jnp.stack([chip, core, pa * 1024]).astype(jnp.int32)
    place = jnp.asarray(np.stack([positions(seq) for seq in SEQ]))

    mine = screening[0]
    swapped = core_swap(mine)
    streams = []
    for part in range(3):
        rows = slice(16 * part, 16 * part + 16)
        streams.append(jnp.concatenate([conduction[:, rows], weighted[:, rows]], axis=1))
    streams = [gathered(block, seq) for block, seq in zip(streams, SEQ)]
    val = gathered(valence, SEQ[3])
    others = [core_swap(block[:, :16]) for block in streams]
    first = core == 0
    partner = jnp.where(first, partner, partner[::-1])
    terms = apply(partner, me, place, streams, others, val, mine, swapped)
    terms = terms.reshape(4, 8, 48, 64)
    terms = spread([terms[k] for k in range(4)], "y", (1, 3, 2))
    terms = terms.reshape(4, 2, 48, 64)
    terms = spread([terms[k] for k in range(4)], "z", (1, 3, 2))
    near = send(terms[1], [(0, 0, 1, 0)] * 2)
    wrap = send(terms[1], [(0, 0, 3, 0)] * 2)
    far = send(terms[0], [(0, 0, 2, 0)] * 2)
    return ((terms[0] + far) + (near + wrap))[None]


def solution(mesh):
    in_specs = (
        P("ka", None, None),
        P("ka", None, None),
        P("ka", None, "pa"),
        P("ka", None, "pa"),
        P(),
        P(),
    )
    out_specs = P("ka", None, None)
    return jax.shard_map(shards, mesh=mesh, in_specs=in_specs, out_specs=out_specs, check_vma=False)
```

```python
import functools
import itertools

import jax
import jax.numpy as jnp
import numpy as np
from jax import lax
from jax.experimental import pallas as pl
from jax.experimental.pallas import tpu as pltpu
from jax.sharding import PartitionSpec as P


NY, NZ, NX = 4, 4, 4
CHIPS = 32
AXES = ("ka", "pa")
STEPS = {
    "y": ("y", 1, 3),
    "Y": ("y", 3, 1),
    "z": ("z", 1, 3),
    "Z": ("z", 3, 1),
    "x": ("x", 1, 3),
    "v": ("x", 1, 1),
}
SEQ = ("ZYzyx", "ZYyxz", "ZYxzy", "vZYzy")
HALF = CHIPS // 2


def device(y, z, x, core):
    return (((y * NZ + z) * 2 + x % 2) * 2 + core) * 2 + x // 2


def moved(masks):
    pairs = []
    for y, z, x, core in itertools.product(range(NY), range(NZ), range(NX), range(2)):
        my, mz, mx, mc = masks[core]
        pairs.append((device(y, z, x, core), device(y ^ my, z ^ mz, x ^ mx, core ^ mc)))
    return pairs


def send(value, masks):
    return lax.ppermute(value, AXES, moved(masks))


def step(value, letter):
    dim, *per_core = STEPS[letter]
    return send(value, [tuple(mask if dim == name else 0 for name in "yzx") + (0,) for mask in per_core])


def core_swap(value):
    return send(value, [(0, 0, 0, 1)] * 2)


def offsets(seq):
    table = np.zeros((2, CHIPS), np.int32)
    for core in range(2):
        for place in range(CHIPS):
            off = {"y": 0, "z": 0, "x": 0}
            for bit, letter in enumerate(seq):
                if place >> bit & 1:
                    off[STEPS[letter][0]] ^= STEPS[letter][1 + core]
            table[core, place] = off["y"] * 8 + off["z"] * 2 + (off["x"] & 1)
    return table


def screen_kernel(parts, rows, *refs):
    count = len(parts)
    given = [refs[11 * n : 11 * n + 11] for n in range(count)]
    screening = refs[11 * count : 11 * count + 2]
    out, mates, weights, dens, slots, msem, wsem, ssem = refs[11 * count + 2 :]
    column = pl.multiple_of(rows[192], 128)

    def load_slot(slot, cut):
        source = screening[slot].at[:, pl.ds(pl.multiple_of(cut * 256, 256), 256)]
        return pltpu.make_async_copy(source, slots.at[slot, cut], ssem.at[slot, cut])

    def load(n):
        for source, first, size in zip(given[n], (0, 8, 16, 24, 32, 48, 56), (8, 8, 8, 8, 16, 8, 8)):
            pltpu.make_async_copy(source, mates.at[n % 2, pl.ds(first, size)], msem.at[n % 2]).start()
        for k in range(4):
            pltpu.make_async_copy(given[n][7 + k], weights.at[n % 2, pl.ds(8 * k, 8)], wsem.at[n % 2]).start()

    def loaded(n):
        pltpu.make_async_copy(mates.at[n % 2], mates.at[n % 2], msem.at[n % 2]).wait()
        pltpu.make_async_copy(weights.at[n % 2], weights.at[n % 2], wsem.at[n % 2]).wait()

    load(0)
    for cut in range(4):
        for slot in range(2):
            load_slot(slot, cut).start()
    if count > 1:
        load(1)

    def pick(turn, slot, unit, cols):
        n = turn // 2
        where = rows[slot * 96 + parts[n] * 32 + (turn % 2) * HALF + unit]
        return mates[n % 2, where, :, cols]

    def build(turn, unit):
        weight = weights[(turn // 2) % 2, (turn % 2) * HALF + unit]
        for slot in range(2):
            here = pl.ds(pl.multiple_of(unit * 16, 16), 16)
            dens[turn % 2, slot, here, :] = pick(turn, slot, unit, slice(None)) * weight

    loaded(0)

    @pl.loop(0, HALF)
    def _(unit):
        build(0, unit)

    for turn in range(2 * count):
        if turn % 2 and turn + 1 < 2 * count:
            loaded((turn + 1) // 2)

        @pl.loop(0, 4)
        def _(cut):
            if turn == 0:
                for slot in range(2):
                    load_slot(slot, cut).wait()
            if turn + 1 < 2 * count:
                for unit in range(4):
                    build(turn + 1, cut * 4 + unit)
            cols = pl.ds(pl.multiple_of(cut * 256, 256), 256)
            here = pl.ds(pl.multiple_of(column + cut * 256, 128), 256)
            screened = [
                jnp.dot(dens[turn % 2, slot], slots[slot, cut], preferred_element_type=jnp.float32)
                for slot in range(2)
            ]
            for unit in range(HALF):
                block = slice(unit * 16, unit * 16 + 16)
                acc = None
                for slot in range(2):
                    term = pick(turn, slot, unit, here).astype(jnp.float32) * screened[slot][block]
                    acc = term if acc is None else acc + term
                out[turn // 2, (turn % 2) * HALF + unit, :, cols] = acc

        if turn % 2 and turn // 2 + 2 < count:
            load(turn // 2 + 2)


def screen(parts, rows, sources, wa, wb):
    vmem = pl.BlockSpec(memory_space=pltpu.VMEM)
    anywhere = pl.BlockSpec(memory_space=pl.ANY)
    count = len(parts)
    return pl.pallas_call(
        functools.partial(screen_kernel, parts),
        grid_spec=pltpu.PrefetchScalarGridSpec(
            num_scalar_prefetch=1,
            grid=(),
            in_specs=[anywhere] * (11 * count + 2),
            out_specs=vmem,
            scratch_shapes=[
                pltpu.VMEM((2, 2 * CHIPS, 16, 2048), jnp.bfloat16),
                pltpu.VMEM((2, CHIPS, 16, 2048), jnp.bfloat16),
                pltpu.VMEM((2, 2, HALF * 16, 2048), jnp.bfloat16),
                pltpu.VMEM((2, 4, 2048, 256), jnp.bfloat16),
                pltpu.SemaphoreType.DMA((2,)),
                pltpu.SemaphoreType.DMA((2,)),
                pltpu.SemaphoreType.DMA((2, 4)),
            ],
        ),
        out_shape=jax.ShapeDtypeStruct((count, CHIPS, 16, 1024), jnp.float32),
        compiler_params=pltpu.CompilerParams(vmem_limit_bytes=50 << 20),
        cost_estimate=pl.CostEstimate(flops=4_300_000_000 * count, bytes_accessed=8 << 20, transcendentals=0),
    )(rows, *sources, wa, wb)


def project_kernel(place, f0, f12, v0, v1, v2, v3, *outs):
    folded = (f0.at[0], f12.at[0], f12.at[1])

    def pick(where):
        slot, kind = lax.bitwise_and(where, 7), where // 8
        odd = lax.bitwise_and(kind, 1) == 1
        return jnp.where(kind < 2, jnp.where(odd, v1[slot], v0[slot]), jnp.where(odd, v3[slot], v2[slot]))

    for group in (1, 3, 2, 0):

        @pl.loop(0, 8, unroll=4)
        def _(unit):
            off = group * 8 + unit
            wide = jnp.concatenate([folded[part][place[part * 32 + off]] for part in range(3)], axis=0)
            high = wide.astype(jnp.bfloat16)
            low = (wide - high.astype(jnp.float32)).astype(jnp.bfloat16)
            left = jnp.concatenate([high, low], axis=0)
            bands = pick(place[96 + off])
            both = lax.dot_general(left, bands, (((1,), (1,)), ((), ())), preferred_element_type=jnp.float32)
            terms = both[:48] + both[48:]
            outs[group][unit] = jnp.concatenate([terms[:24], terms[24:]], axis=1)


def project(place, folded, val):
    vmem = pl.BlockSpec(memory_space=pltpu.VMEM)
    return pl.pallas_call(
        project_kernel,
        grid_spec=pltpu.PrefetchScalarGridSpec(
            num_scalar_prefetch=1, grid=(), in_specs=[vmem] * 6, out_specs=[vmem] * 4
        ),
        out_shape=[jax.ShapeDtypeStruct((8, 24, 128), jnp.float32)] * 4,
        compiler_params=pltpu.CompilerParams(vmem_limit_bytes=14 << 20),
        cost_estimate=pl.CostEstimate(flops=800_000_000, bytes_accessed=10 << 20, transcendentals=0),
    )(place, *folded, *val)


def spread(parts, dim, masks):
    moves = []
    for mask in masks:
        one = tuple(mask if dim == name else 0 for name in "yzx") + (0,)
        moves.append(send(parts[mask], [one] * 2))
    return (parts[0] + moves[0]) + (moves[1] + moves[2])


def lookup(keys, table):
    spots = jnp.arange(table.shape[-1], dtype=jnp.int32)
    return jnp.sum(jnp.where(keys[..., None] == spots, table[..., None, :], 0), axis=-1)


def tables(chip, core, pa, pair_transfer, owner_map):
    owned = lax.dynamic_slice_in_dim(owner_map, chip * 2, 2)
    owned = jnp.where(core == 0, owned, owned[::-1])
    columns = jnp.arange(pair_transfer.shape[1], dtype=jnp.int32)
    partner = jnp.sum(jnp.where(pair_transfer[None] == owned[:, None, None], columns, 0), axis=2)
    offs = np.stack([offsets(seq) for seq in SEQ])
    place = np.argsort(offs, axis=-1).astype(np.int32)
    mine = lambda table: jnp.where(core == 0, table[:, 0], table[:, 1])
    home = lax.bitwise_xor(mine(offs[:3]), chip) * 2 + core
    mates = lookup(jnp.broadcast_to(home, (2, 3, CHIPS)), partner[:, None, :])
    key = lax.bitwise_xor(mates & 1, core) * CHIPS + lax.bitwise_xor(mates >> 1, chip)
    both = np.stack([np.concatenate([place[:3, c], CHIPS + place[:3, 1 - c]], -1) for c in (0, 1)], 1)
    rows = lookup(key, mine(both)[None])
    rows = jnp.concatenate([rows.reshape(-1), (pa * 1024).astype(jnp.int32)[None]])
    return rows, mine(place).reshape(-1)


def shards(conduction, weighted, valence, screening, pair_transfer, owner_map):
    ka, pa = lax.axis_index("ka"), lax.axis_index("pa")
    chip, core = ka // 2, ka % 2
    rows, place = tables(chip, core, pa, pair_transfer, owner_map)
    mine = screening[0]

    stream = jnp.concatenate([conduction, weighted], axis=1)
    val = [valence]
    for turn in range(2):
        moves = [step(stream, SEQ[0][turn]), step(val[0], SEQ[3][turn])]
        stream, val, moves = lax.optimization_barrier((stream, val, moves))
        stream = jnp.concatenate([stream, moves[0]], axis=0)
        val = [jnp.concatenate([val[0], moves[1]], axis=0)]
    parts = [slice(16 * part, 16 * part + 16) for part in range(3)]
    streams = [jnp.concatenate([stream[:, :48][:, cut], stream[:, 48:][:, cut]], axis=1) for cut in parts]
    moves = [step(block, SEQ[k][2]) for k, block in enumerate(streams)]
    val_move = step(val[0], SEQ[3][2])
    streams, moves = lax.optimization_barrier((streams, moves))
    cond = [[jnp.concatenate([one[:, :16], two[:, :16]], axis=0)] for one, two in zip(streams, moves)]
    weights = [[jnp.concatenate([one[:, 16:], two[:, 16:]], axis=0)] for one, two in zip(streams, moves)]

    def onward(pieces, source, turn):
        for k, held in enumerate(pieces):
            held.append(step(held[source], SEQ[k][turn]))

    onward(cond, 0, 3)
    onward(cond, 0, 4)
    onward(cond, 1, 4)
    onward(weights, 0, 3)
    onward(weights, 0, 4)
    onward(weights, 1, 4)
    val = jnp.concatenate([val[0], val_move], axis=0)
    swapped = core_swap(mine)
    val_next, val_far = step(val, SEQ[3][3]), step(val, SEQ[3][4])
    others = []
    for held in cond:
        both = [jnp.concatenate(held[:2], axis=0), held[2], held[3]]
        others.append([core_swap(block) for block in both])
    inputs = [held + other + weight for held, other, weight in zip(cond, others, weights)]
    first = screen((0,), rows, inputs[0], mine, swapped)
    first, val_next = lax.optimization_barrier((first, val_next))
    val_last = step(val_next, SEQ[3][4])
    folded = [first, screen((1, 2), rows, inputs[1] + inputs[2], mine, swapped)]
    folded, val_last = lax.optimization_barrier((folded, val_last))
    terms = project(place, folded, (val, val_next, val_far, val_last))
    terms = spread(terms, "y", (1, 3, 2))
    terms = terms.reshape(4, 2, 24, 128)
    terms = spread([terms[k] for k in range(4)], "z", (1, 3, 2))
    near = send(terms[1], [(0, 0, 1, 0)] * 2)
    wrap = send(terms[1], [(0, 0, 3, 0)] * 2)
    across = send(terms[0], [(0, 0, 2, 0)] * 2)
    total = (terms[0] + across) + (near + wrap)
    return jnp.concatenate([total[:, :64], total[:, 64:]], axis=0)[None]


def solution(mesh):
    in_specs = (
        P("ka", None, None),
        P("ka", None, None),
        P("ka", None, "pa"),
        P("ka", None, "pa"),
        P(),
        P(),
    )
    out_specs = P("ka", None, None)
    return jax.shard_map(shards, mesh=mesh, in_specs=in_specs, out_specs=out_specs, check_vma=False)
```

```python
import functools
import itertools

import jax
import jax.numpy as jnp
import numpy as np
from jax import lax
from jax.experimental import pallas as pl
from jax.experimental.pallas import tpu as pltpu
from jax.sharding import PartitionSpec as P


NY, NZ, NX = 4, 4, 4
CHIPS = 32
AXES = ("ka", "pa")
STEPS = {
    "y": ("y", 1, 3),
    "Y": ("y", 3, 1),
    "z": ("z", 1, 3),
    "Z": ("z", 3, 1),
    "x": ("x", 1, 3),
    "v": ("x", 1, 1),
}
SEQ = ("ZYzyx", "ZYyxz", "ZYxzy", "vZYzy")
HALF = CHIPS // 2

def device(y, z, x, core):
    return (((y * NZ + z) * 2 + x % 2) * 2 + core) * 2 + x // 2

def moved(masks):
    pairs = []
    for y, z, x, core in itertools.product(range(NY), range(NZ), range(NX), range(2)):
        my, mz, mx, mc = masks[core]
        pairs.append((device(y, z, x, core), device(y ^ my, z ^ mz, x ^ mx, core ^ mc)))
    return pairs

def send(value, masks):
    return lax.ppermute(value, AXES, moved(masks))

def step(value, letter):
    dim, *per_core = STEPS[letter]
    return send(value, [tuple(mask if dim == name else 0 for name in "yzx") + (0,) for mask in per_core])

def core_swap(value):
    return send(value, [(0, 0, 0, 1)] * 2)

def offsets(seq):
    table = np.zeros((2, CHIPS), np.int32)
    for core in range(2):
        for place in range(CHIPS):
            off = {"y": 0, "z": 0, "x": 0}
            for bit, letter in enumerate(seq):
                if place >> bit & 1:
                    off[STEPS[letter][0]] ^= STEPS[letter][1 + core]
            table[core, place] = off["y"] * 8 + off["z"] * 2 + (off["x"] & 1)
    return table

def screen_kernel(parts, rows, *refs):
    count = len(parts)
    given = [refs[8 * n : 8 * n + 8] for n in range(count)]
    screening = refs[8 * count : 8 * count + 2]
    out, mates, weights, dens, slots, msem, wsem, ssem = refs[8 * count + 2 :]
    column = pl.multiple_of(rows[192], 128)

    def load_slot(slot, cut):
        source = screening[slot].at[:, pl.ds(pl.multiple_of(cut * 256, 256), 256)]
        return pltpu.make_async_copy(source, slots.at[slot, cut], ssem.at[slot, cut])

    def load(n):
        for k in range(8):
            rows_of = pl.ds(8 * k, 8)
            if k < 4:
                bands = given[n][k].at[:, pl.ds(16, 16)]
                pltpu.make_async_copy(bands, weights.at[n % 2, rows_of], wsem.at[n % 2]).start()
            pltpu.make_async_copy(given[n][k].at[:, pl.ds(0, 16)], mates.at[n % 2, rows_of], msem.at[n % 2]).start()

    def loaded(n):
        pltpu.make_async_copy(mates.at[n % 2], mates.at[n % 2], msem.at[n % 2]).wait()
        pltpu.make_async_copy(weights.at[n % 2], weights.at[n % 2], wsem.at[n % 2]).wait()

    load(0)
    for cut in range(4):
        for slot in range(2):
            load_slot(slot, cut).start()
    if count > 1:
        load(1)

    def pick(turn, slot, unit, cols):
        n = turn // 2
        where = rows[slot * 96 + parts[n] * 32 + (turn % 2) * HALF + unit]
        return mates[n % 2, where, :, cols]

    def build(turn, unit):
        weight = weights[(turn // 2) % 2, (turn % 2) * HALF + unit]
        for slot in range(2):
            here = pl.ds(pl.multiple_of(unit * 16, 16), 16)
            dens[turn % 2, slot, here, :] = pick(turn, slot, unit, slice(None)) * weight

    loaded(0)

    @pl.loop(0, HALF)
    def _(unit):
        build(0, unit)

    for turn in range(2 * count):
        if turn % 2 and turn + 1 < 2 * count:
            loaded((turn + 1) // 2)

        @pl.loop(0, 4)
        def _(cut):
            if turn == 0:
                for slot in range(2):
                    load_slot(slot, cut).wait()
            if turn + 1 < 2 * count:
                for unit in range(4):
                    build(turn + 1, cut * 4 + unit)
            cols = pl.ds(pl.multiple_of(cut * 256, 256), 256)
            here = pl.ds(pl.multiple_of(column + cut * 256, 128), 256)
            screened = [
                jnp.dot(dens[turn % 2, slot], slots[slot, cut], preferred_element_type=jnp.float32)
                for slot in range(2)
            ]
            for unit in range(HALF):
                block = slice(unit * 16, unit * 16 + 16)
                acc = None
                for slot in range(2):
                    term = pick(turn, slot, unit, here).astype(jnp.float32) * screened[slot][block]
                    acc = term if acc is None else acc + term
                out[turn // 2, (turn % 2) * HALF + unit, :, cols] = acc

        if turn % 2 and turn // 2 + 2 < count:
            load(turn // 2 + 2)

def screen(parts, rows, sources, wa, wb):
    vmem = pl.BlockSpec(memory_space=pltpu.VMEM)
    anywhere = pl.BlockSpec(memory_space=pl.ANY)
    count = len(parts)
    return pl.pallas_call(
        functools.partial(screen_kernel, parts),
        grid_spec=pltpu.PrefetchScalarGridSpec(
            num_scalar_prefetch=1,
            grid=(),
            in_specs=[anywhere] * (8 * count + 2),
            out_specs=vmem,
            scratch_shapes=[
                pltpu.VMEM((min(count, 2), 2 * CHIPS, 16, 2048), jnp.bfloat16),
                pltpu.VMEM((min(count, 2), CHIPS, 16, 2048), jnp.bfloat16),
                pltpu.VMEM((2, 2, HALF * 16, 2048), jnp.bfloat16),
                pltpu.VMEM((2, 4, 2048, 256), jnp.bfloat16),
                pltpu.SemaphoreType.DMA((2,)),
                pltpu.SemaphoreType.DMA((2,)),
                pltpu.SemaphoreType.DMA((2, 4)),
            ],
        ),
        out_shape=jax.ShapeDtypeStruct((count, CHIPS, 16, 1024), jnp.float32),
        compiler_params=pltpu.CompilerParams(vmem_limit_bytes=46 << 20),
        cost_estimate=pl.CostEstimate(flops=4_300_000_000 * count, bytes_accessed=8 << 20, transcendentals=0),
    )(rows, *sources, wa, wb)

def project_kernel(place, f0, f21, v0, v1, v2, v3, *outs):
    folded = (f0.at[0], f21.at[1], f21.at[0])

    def pick(where):
        slot, kind = lax.bitwise_and(where, 7), where // 8
        odd = lax.bitwise_and(kind, 1) == 1
        return jnp.where(kind < 2, jnp.where(odd, v1[slot], v0[slot]), jnp.where(odd, v3[slot], v2[slot]))

    for group in (1, 3, 2, 0):

        @pl.loop(0, 8, unroll=4)
        def _(unit):
            off = group * 8 + unit
            wide = jnp.concatenate([folded[part][place[part * 32 + off]] for part in range(3)], axis=0)
            high = wide.astype(jnp.bfloat16)
            low = (wide - high.astype(jnp.float32)).astype(jnp.bfloat16)
            left = jnp.concatenate([high, low], axis=0)
            bands = pick(place[96 + off])
            both = lax.dot_general(left, bands, (((1,), (1,)), ((), ())), preferred_element_type=jnp.float32)
            terms = both[:48] + both[48:]
            outs[group][unit] = jnp.concatenate([terms[:24], terms[24:]], axis=1)

def project(place, folded, val):
    vmem = pl.BlockSpec(memory_space=pltpu.VMEM)
    return pl.pallas_call(
        project_kernel,
        grid_spec=pltpu.PrefetchScalarGridSpec(
            num_scalar_prefetch=1, grid=(), in_specs=[vmem] * 6, out_specs=[vmem] * 4
        ),
        out_shape=[jax.ShapeDtypeStruct((8, 24, 128), jnp.float32)] * 4,
        compiler_params=pltpu.CompilerParams(vmem_limit_bytes=14 << 20),
        cost_estimate=pl.CostEstimate(flops=800_000_000, bytes_accessed=10 << 20, transcendentals=0),
    )(place, *folded, *val)

def spread(parts, dim, masks):
    moves = []
    for mask in masks:
        one = tuple(mask if dim == name else 0 for name in "yzx") + (0,)
        moves.append(send(parts[mask], [one] * 2))
    return (parts[0] + moves[0]) + (moves[1] + moves[2])

def lookup(keys, table):
    spots = jnp.arange(table.shape[-1], dtype=jnp.int32)
    return jnp.sum(jnp.where(keys[..., None] == spots, table[..., None, :], 0), axis=-1)

def tables(chip, core, pa, pair_transfer, owner_map):
    owned = lax.dynamic_slice_in_dim(owner_map, chip * 2, 2)
    owned = jnp.where(core == 0, owned, owned[::-1])
    columns = jnp.arange(pair_transfer.shape[1], dtype=jnp.int32)
    partner = jnp.sum(jnp.where(pair_transfer[None] == owned[:, None, None], columns, 0), axis=2)
    offs = np.stack([offsets(seq) for seq in SEQ])
    place = np.argsort(offs, axis=-1).astype(np.int32)
    mine = lambda table: jnp.where(core == 0, table[:, 0], table[:, 1])
    home = lax.bitwise_xor(mine(offs[:3]), chip) * 2 + core
    mates = lookup(jnp.broadcast_to(home, (2, 3, CHIPS)), partner[:, None, :])
    key = lax.bitwise_xor(mates & 1, core) * CHIPS + lax.bitwise_xor(mates >> 1, chip)
    both = np.stack([np.concatenate([place[:3, c], CHIPS + place[:3, 1 - c]], -1) for c in (0, 1)], 1)
    rows = lookup(key, mine(both)[None])
    rows = jnp.concatenate([rows.reshape(-1), (pa * 1024).astype(jnp.int32)[None]])
    return rows, mine(place).reshape(-1)

def shards(conduction, weighted, valence, screening, pair_transfer, owner_map):
    ka, pa = lax.axis_index("ka"), lax.axis_index("pa")
    chip, core = ka // 2, ka % 2
    rows, place = tables(chip, core, pa, pair_transfer, owner_map)
    mine = screening[0]

    stream = jnp.concatenate([conduction, weighted], axis=1)
    units = [stream, step(stream, "Z"), step(stream, "Y")]
    units.append(step(units[1], "Y"))
    val = jnp.concatenate([valence, step(valence, SEQ[3][0])], axis=0)
    units = lax.optimization_barrier(units)
    streams = []
    for part in range(3):
        cut, low = slice(16 * part, 16 * part + 16), slice(48 + 16 * part, 64 + 16 * part)
        streams.append(jnp.concatenate([jnp.concatenate([one[:, cut], one[:, low]], axis=1) for one in units], axis=0))
    moves = [step(block, SEQ[k][2]) for k, block in enumerate(streams)]
    val_move = step(val, SEQ[3][1])
    streams, moves = lax.optimization_barrier((streams, moves))
    pieces = [[jnp.concatenate(pair, axis=0)] for pair in zip(streams, moves)]
    for source, turn in ((0, 3), (0, 4), (1, 4)):
        for k, held in enumerate(pieces):
            held.append(step(held[source], SEQ[k][turn]))
    val = jnp.concatenate([val, val_move], axis=0)
    val = jnp.concatenate([val, step(val, SEQ[3][2])], axis=0)
    swapped = core_swap(mine)
    val_next, val_far = step(val, SEQ[3][3]), step(val, SEQ[3][4])
    val_last = step(val_next, SEQ[3][4])
    inputs = []
    for held in pieces:
        inputs.append(held + [core_swap(block) for block in held])
    folded = [screen((0,), rows, inputs[0], mine, swapped)]
    folded.append(screen((2, 1), rows, inputs[2] + inputs[1], mine, swapped))
    folded, val_last = lax.optimization_barrier((folded, val_last))
    terms = project(place, folded, (val, val_next, val_far, val_last))
    terms = spread(terms, "y", (1, 3, 2))
    terms = terms.reshape(4, 2, 24, 128)
    terms = spread([terms[k] for k in range(4)], "z", (1, 3, 2))
    near = send(terms[1], [(0, 0, 1, 0)] * 2)
    wrap = send(terms[1], [(0, 0, 3, 0)] * 2)
    across = send(terms[0], [(0, 0, 2, 0)] * 2)
    total = (terms[0] + across) + (near + wrap)
    return jnp.concatenate([total[:, :64], total[:, 64:]], axis=0)[None]

def solution(mesh):
    in_specs = (
        P("ka", None, None),
        P("ka", None, None),
        P("ka", None, "pa"),
        P("ka", None, "pa"),
        P(),
        P(),
    )
    out_specs = P("ka", None, None)
    return jax.shard_map(shards, mesh=mesh, in_specs=in_specs, out_specs=out_specs, check_vma=False)
```

```python
import functools
import itertools

import jax
import jax.numpy as jnp
import numpy as np
from jax import lax
from jax.experimental import pallas as pl
from jax.experimental.pallas import tpu as pltpu
from jax.sharding import PartitionSpec as P


NY, NZ, NX = 4, 4, 4
CHIPS = 32
AXES = ("ka", "pa")
STEPS = {
    "y": ("y", 1, 3),
    "Y": ("y", 3, 1),
    "z": ("z", 1, 3),
    "Z": ("z", 3, 1),
    "x": ("x", 1, 3),
    "v": ("x", 1, 1),
}
SEQ = ("ZYzyx", "ZYyxz", "ZYxzy", "vZYzy")
HALF = CHIPS // 2

def device(y, z, x, core):
    return (((y * NZ + z) * 2 + x % 2) * 2 + core) * 2 + x // 2

def moved(masks):
    pairs = []
    for y, z, x, core in itertools.product(range(NY), range(NZ), range(NX), range(2)):
        my, mz, mx, mc = masks[core]
        pairs.append((device(y, z, x, core), device(y ^ my, z ^ mz, x ^ mx, core ^ mc)))
    return pairs

def send(value, masks):
    return lax.ppermute(value, AXES, moved(masks))

def step(value, letter):
    dim, *per_core = STEPS[letter]
    return send(value, [tuple(mask if dim == name else 0 for name in "yzx") + (0,) for mask in per_core])

def core_swap(value):
    return send(value, [(0, 0, 0, 1)] * 2)

def offsets(seq):
    table = np.zeros((2, CHIPS), np.int32)
    for core in range(2):
        for place in range(CHIPS):
            off = {"y": 0, "z": 0, "x": 0}
            for bit, letter in enumerate(seq):
                if place >> bit & 1:
                    off[STEPS[letter][0]] ^= STEPS[letter][1 + core]
            table[core, place] = off["y"] * 8 + off["z"] * 2 + (off["x"] & 1)
    return table

def screen_kernel(parts, rows, *refs):
    count = len(parts)
    given = [refs[8 * n : 8 * n + 8] for n in range(count)]
    screening = refs[8 * count : 8 * count + 2]
    out, mates, weights, dens, slots, msem, wsem, ssem = refs[8 * count + 2 :]
    column = pl.multiple_of(rows[192], 128)

    def load_slot(slot, cut):
        source = screening[slot].at[:, pl.ds(pl.multiple_of(cut * 256, 256), 256)]
        return pltpu.make_async_copy(source, slots.at[slot, cut], ssem.at[slot, cut])

    def load(n):
        for k in range(8):
            rows_of = pl.ds(8 * k, 8)
            if k < 4:
                bands = given[n][k].at[:, pl.ds(16, 16)]
                pltpu.make_async_copy(bands, weights.at[n % 2, rows_of], wsem.at[n % 2]).start()
            pltpu.make_async_copy(given[n][k].at[:, pl.ds(0, 16)], mates.at[n % 2, rows_of], msem.at[n % 2]).start()

    def loaded(n):
        pltpu.make_async_copy(mates.at[n % 2], mates.at[n % 2], msem.at[n % 2]).wait()
        pltpu.make_async_copy(weights.at[n % 2], weights.at[n % 2], wsem.at[n % 2]).wait()

    load(0)
    for cut in range(4):
        for slot in range(2):
            load_slot(slot, cut).start()
    if count > 1:
        load(1)

    def pick(turn, slot, unit, cols):
        n = turn // 2
        where = rows[slot * 96 + parts[n] * 32 + (turn % 2) * HALF + unit]
        return mates[n % 2, where, :, cols]

    def build(turn, unit):
        weight = weights[(turn // 2) % 2, (turn % 2) * HALF + unit]
        for slot in range(2):
            here = pl.ds(pl.multiple_of(unit * 16, 16), 16)
            dens[turn % 2, slot, here, :] = pick(turn, slot, unit, slice(None)) * weight

    loaded(0)

    @pl.loop(0, HALF)
    def _(unit):
        build(0, unit)

    for turn in range(2 * count):
        if turn % 2 and turn + 1 < 2 * count:
            loaded((turn + 1) // 2)

        @pl.loop(0, 4)
        def _(cut):
            if turn == 0:
                for slot in range(2):
                    load_slot(slot, cut).wait()
            if turn + 1 < 2 * count:
                for unit in range(4):
                    build(turn + 1, cut * 4 + unit)
            cols = pl.ds(pl.multiple_of(cut * 256, 256), 256)
            here = pl.ds(pl.multiple_of(column + cut * 256, 128), 256)
            screened = [
                jnp.dot(dens[turn % 2, slot], slots[slot, cut], preferred_element_type=jnp.float32)
                for slot in range(2)
            ]
            for unit in range(HALF):
                block = slice(unit * 16, unit * 16 + 16)
                acc = None
                for slot in range(2):
                    term = pick(turn, slot, unit, here).astype(jnp.float32) * screened[slot][block]
                    acc = term if acc is None else acc + term
                out[turn // 2, (turn % 2) * HALF + unit, :, cols] = acc

        if turn % 2 and turn // 2 + 2 < count:
            load(turn // 2 + 2)

def screen(parts, rows, sources, wa, wb):
    vmem = pl.BlockSpec(memory_space=pltpu.VMEM)
    anywhere = pl.BlockSpec(memory_space=pl.ANY)
    count = len(parts)
    return pl.pallas_call(
        functools.partial(screen_kernel, parts),
        grid_spec=pltpu.PrefetchScalarGridSpec(
            num_scalar_prefetch=1,
            grid=(),
            in_specs=[anywhere] * (8 * count + 2),
            out_specs=vmem,
            scratch_shapes=[
                pltpu.VMEM((min(count, 2), 2 * CHIPS, 16, 2048), jnp.bfloat16),
                pltpu.VMEM((min(count, 2), CHIPS, 16, 2048), jnp.bfloat16),
                pltpu.VMEM((2, 2, HALF * 16, 2048), jnp.bfloat16),
                pltpu.VMEM((2, 4, 2048, 256), jnp.bfloat16),
                pltpu.SemaphoreType.DMA((2,)),
                pltpu.SemaphoreType.DMA((2,)),
                pltpu.SemaphoreType.DMA((2, 4)),
            ],
        ),
        out_shape=jax.ShapeDtypeStruct((count, CHIPS, 16, 1024), jnp.float32),
        compiler_params=pltpu.CompilerParams(vmem_limit_bytes=46 << 20),
        cost_estimate=pl.CostEstimate(flops=4_300_000_000 * count, bytes_accessed=8 << 20, transcendentals=0),
    )(rows, *sources, wa, wb)

def project_kernel(place, f0, f21, v0, v1, v2, v3, *outs):
    folded = (f0.at[0], f21.at[1], f21.at[0])

    def pick(where):
        slot, kind = lax.bitwise_and(where, 7), where // 8
        odd = lax.bitwise_and(kind, 1) == 1
        return jnp.where(kind < 2, jnp.where(odd, v1[slot], v0[slot]), jnp.where(odd, v3[slot], v2[slot]))

    for group in (1, 3, 2, 0):

        @pl.loop(0, 8, unroll=4)
        def _(unit):
            off = group * 8 + unit
            wide = jnp.concatenate([folded[part][place[part * 32 + off]] for part in range(3)], axis=0)
            high = wide.astype(jnp.bfloat16)
            low = (wide - high.astype(jnp.float32)).astype(jnp.bfloat16)
            left = jnp.concatenate([high, low], axis=0)
            bands = pick(place[96 + off])
            both = lax.dot_general(left, bands, (((1,), (1,)), ((), ())), preferred_element_type=jnp.float32)
            terms = both[:48] + both[48:]
            outs[group][unit] = jnp.concatenate([terms[:24], terms[24:]], axis=1).astype(outs[group].dtype)

def project(place, folded, val):
    vmem = pl.BlockSpec(memory_space=pltpu.VMEM)
    return pl.pallas_call(
        project_kernel,
        grid_spec=pltpu.PrefetchScalarGridSpec(
            num_scalar_prefetch=1, grid=(), in_specs=[vmem] * 6, out_specs=[vmem] * 4
        ),
        out_shape=[jax.ShapeDtypeStruct((8, 24, 128), jnp.bfloat16 if k else jnp.float32) for k in range(4)],
        compiler_params=pltpu.CompilerParams(vmem_limit_bytes=14 << 20),
        cost_estimate=pl.CostEstimate(flops=800_000_000, bytes_accessed=10 << 20, transcendentals=0),
    )(place, *folded, *val)

def spread(parts, dim, masks):
    moves = []
    for mask in masks:
        one = tuple(mask if dim == name else 0 for name in "yzx") + (0,)
        moves.append(send(parts[mask], [one] * 2).astype(jnp.float32))
    return (parts[0] + moves[0]) + (moves[1] + moves[2])

def lookup(keys, table):
    spots = jnp.arange(table.shape[-1], dtype=jnp.int32)
    return jnp.sum(jnp.where(keys[..., None] == spots, table[..., None, :], 0), axis=-1)

def tables(chip, core, pa, pair_transfer, owner_map):
    owned = lax.dynamic_slice_in_dim(owner_map, chip * 2, 2)
    owned = jnp.where(core == 0, owned, owned[::-1])
    columns = jnp.arange(pair_transfer.shape[1], dtype=jnp.int32)
    partner = jnp.sum(jnp.where(pair_transfer[None] == owned[:, None, None], columns, 0), axis=2)
    offs = np.stack([offsets(seq) for seq in SEQ])
    place = np.argsort(offs, axis=-1).astype(np.int32)
    mine = lambda table: jnp.where(core == 0, table[:, 0], table[:, 1])
    home = lax.bitwise_xor(mine(offs[:3]), chip) * 2 + core
    mates = lookup(jnp.broadcast_to(home, (2, 3, CHIPS)), partner[:, None, :])
    key = lax.bitwise_xor(mates & 1, core) * CHIPS + lax.bitwise_xor(mates >> 1, chip)
    both = np.stack([np.concatenate([place[:3, c], CHIPS + place[:3, 1 - c]], -1) for c in (0, 1)], 1)
    rows = lookup(key, mine(both)[None])
    rows = jnp.concatenate([rows.reshape(-1), (pa * 1024).astype(jnp.int32)[None]])
    return rows, mine(place).reshape(-1)

def shards(conduction, weighted, valence, screening, pair_transfer, owner_map):
    ka, pa = lax.axis_index("ka"), lax.axis_index("pa")
    chip, core = ka // 2, ka % 2
    rows, place = tables(chip, core, pa, pair_transfer, owner_map)
    mine = screening[0]

    stream = jnp.concatenate([conduction, weighted], axis=1)
    units = [stream, step(stream, "Z"), step(stream, "Y")]
    units.append(step(units[1], "Y"))
    val = jnp.concatenate([valence, step(valence, SEQ[3][0])], axis=0)
    units = lax.optimization_barrier(units)
    streams = []
    for part in range(3):
        cut, low = slice(16 * part, 16 * part + 16), slice(48 + 16 * part, 64 + 16 * part)
        streams.append(jnp.concatenate([jnp.concatenate([one[:, cut], one[:, low]], axis=1) for one in units], axis=0))
    moves = [step(block, SEQ[k][2]) for k, block in enumerate(streams)]
    val_move = step(val, SEQ[3][1])
    streams, moves = lax.optimization_barrier((streams, moves))
    pieces = [[jnp.concatenate(pair, axis=0)] for pair in zip(streams, moves)]
    for source, turn in ((0, 3), (0, 4), (1, 4)):
        for k, held in enumerate(pieces):
            held.append(step(held[source], SEQ[k][turn]))
    val = jnp.concatenate([val, val_move], axis=0)
    val = jnp.concatenate([val, step(val, SEQ[3][2])], axis=0)
    swapped = core_swap(mine)
    val_next, val_far = step(val, SEQ[3][3]), step(val, SEQ[3][4])
    val_last = step(val_next, SEQ[3][4])
    inputs = []
    for held in pieces:
        inputs.append(held + [core_swap(block) for block in held])
    folded = [screen((0,), rows, inputs[0], mine, swapped)]
    folded.append(screen((2, 1), rows, inputs[2] + inputs[1], mine, swapped))
    folded, val_last = lax.optimization_barrier((folded, val_last))
    terms = project(place, folded, (val, val_next, val_far, val_last))
    terms = spread(terms, "y", (1, 3, 2))
    terms = terms.reshape(4, 2, 24, 128)
    terms = spread([terms[k] for k in range(4)], "z", (1, 3, 2))
    near = send(terms[1], [(0, 0, 1, 0)] * 2)
    wrap = send(terms[1], [(0, 0, 3, 0)] * 2)
    across = send(terms[0], [(0, 0, 2, 0)] * 2)
    total = (terms[0] + across) + (near + wrap)
    return jnp.concatenate([total[:, :64], total[:, 64:]], axis=0)[None]

def solution(mesh):
    in_specs = (
        P("ka", None, None),
        P("ka", None, None),
        P("ka", None, "pa"),
        P("ka", None, "pa"),
        P(),
        P(),
    )
    out_specs = P("ka", None, None)
    return jax.shard_map(shards, mesh=mesh, in_specs=in_specs, out_specs=out_specs, check_vma=False)
```
